32 devices in a mesh: dom: 2 (over y), grid: 4 (over z), band: 2 (over x), mem: 2 (over core).
Axes of the slice: x: 2, y: 2, z: 4, core: 2. Of those that a mesh axis runs over, the one named last changes fastest.
Arguments:
- grid_state: bfloat16 [4, 2048, 128], P(('dom', 'mem'), 'grid'), parts along dimension 0, may hold values from -6 to 6
- forcing: bfloat16 [4096, 128], P(('dom', 'grid')), parts along dimension 0, may hold values from -6 to 6
- boundary_mask: int32 [2048], P('grid'), may hold values 0 or 1
- edge_src: int32 [4, 4, 32], P('grid'), may hold values from 0 to 511
- edge_dst: int32 [4, 4, 32], P(None, 'grid'), may hold values from 0 to 127
- edge_count: int32 [4, 4], P(None, 'grid'), may hold values from 0 to 32, as said below
- edge_weight: float32 [4, 4, 32], P(None, 'grid'), may hold values from 0.1 to 1
- embed_weight: bfloat16 [128, 1024], P(None, 'band'), may hold values from -0.5 to 0.5
- attn_qkv: bfloat16 [1, 1024, 3, 1024], P(None, 'mem', None, 'band'), may hold values from -0.1875 to 0.1875
- attn_out: bfloat16 [1, 1024, 1024], P(None, 'band', 'mem'), may hold values from -0.1875 to 0.1875
- mlp_in: bfloat16 [1, 1024, 4096], P(None, 'mem', 'band'), may hold values from -0.1875 to 0.1875
- mlp_out: bfloat16 [1, 4096, 1024], P(None, 'band', 'mem'), may hold values from -0.09375 to 0.09375
- decode_weight: bfloat16 [1024, 128], P('band'), may hold values from -0.1875 to 0.1875
Outputs:
- next_state: bfloat16 [4, 2048, 128], P(('dom', 'mem'), 'grid'), parts along dimension 0
The draws below stay inside these ranges and needn't reach their ends.
There are 2 independent parts, one for each index of `dom`. The reference program is written for one: setup_inputs(seed, part) draws one part's arguments, and reference() takes and returns one part's arrays. A program takes and returns all parts, laid end to end along the dimension named above; an argument that names none is the same for every part. Nothing has to cross between parts.
Inputs may be any that keep to these rules, and one draw needn't show every extreme that they name: Slots at or beyond edge_count[i, j] in a block are padding. In every draw some mesh band receives 32 live slots from every grid shard.
All inputs are finite; a program needn't handle non-finite values. No bound on the sum of `boundary_mask` on one device may be relied on, other than what follows from the above.
Results may differ from the reference program's by a relative error of at most 0.011.
Values may be sent and summed in bfloat16 or wider, within the bound.
No kernel may reach another device: no remote copies, remote signals or barrier semaphores. Data moves between devices by JAX's collectives and lax.ppermute only.
A program may use at most 64 MiB of HBM per device.

```python
import math
import jax
import jax.numpy as jnp
from jax import lax

D = 1024
HEADS = 16
FF = 4096
CHANNELS = 128
LAYERS = 1
GP_DEV = 512
M_DEV = 128
HEAD_DIM = 64
WINDOW = 64
EDGE_SLOTS = 32
MEMBERS = 2
GRID_POINTS = 2048
MESH_NODES = 512
N_GRID = 4
N_BAND = 2


def draw_edge_count(key, part):
    busiest = jax.random.randint(jax.random.fold_in(key, 7), (), 0, N_GRID)
    counted = jax.random.randint(jax.random.fold_in(key, 11), (N_GRID, N_GRID), 0, EDGE_SLOTS + 1)
    column = jnp.arange(N_GRID, dtype=jnp.int32)[None, :]
    return jnp.where(column == busiest, EDGE_SLOTS, counted).astype(jnp.int32)


def touch_ends(drawn, own_key, least, high):
    spot = [jax.random.randint(jax.random.fold_in(own_key, axis), (), 0, length) for axis, length in enumerate(drawn.shape)]
    main_axis = drawn.shape.index(max(drawn.shape))
    next_to = spot[:main_axis] + [(spot[main_axis] + 1) % drawn.shape[main_axis]] + spot[main_axis + 1:]
    return drawn.at[tuple(spot)].set(least).at[tuple(next_to)].set(high)


def block_levels(own_key, extent, shards, least, high):
    def one(axis_at, parts):
        draws = jax.random.uniform(jax.random.fold_in(jax.random.fold_in(own_key, 6), axis_at), (parts,), jnp.float32, least / len(shards), high / len(shards))
        return jnp.repeat(jnp.exp(draws), extent[axis_at] // parts).reshape((-1,) + (1,) * (len(extent) - axis_at - 1))

    level = one(*shards[0])
    for cut in shards[1:]:
        level = level * one(*cut)
    return level


def noise(own_key, dims, spread, most, cuts=(), kind=jnp.bfloat16):
    values = spread * jax.random.normal(own_key, dims, jnp.float32)
    if cuts:
        values = values * block_levels(own_key, dims, cuts, -0.22, 0.18)
    return jnp.clip(values, -most, most).astype(kind)


def setup_inputs(seed: int = 0, part: int = 0) -> dict:
    key_list = jax.random.split(jax.random.key(seed), 14)
    own_keys = jax.random.split(jax.random.fold_in(key_list[13], part), 14)
    return {
        "grid_state": noise(own_keys[0], (MEMBERS, GRID_POINTS, CHANNELS), 1.0, 6.0, ((0, 2), (1, 4))),
        "forcing": noise(own_keys[1], (GRID_POINTS, CHANNELS), 1.0, 6.0, ((0, 4),)),
        "boundary_mask": touch_ends((jax.random.randint(key_list[2], (GRID_POINTS,), 0, 4) < 1).astype(jnp.int32), jax.random.fold_in(key_list[2], 1), 0, 1),
        "edge_src": touch_ends(jax.random.randint(key_list[3], (N_GRID, N_GRID, EDGE_SLOTS), 0, GP_DEV), jax.random.fold_in(key_list[3], 1), 0, GP_DEV - 1).astype(jnp.int32),
        "edge_dst": touch_ends(jax.random.randint(key_list[4], (N_GRID, N_GRID, EDGE_SLOTS), 0, M_DEV), jax.random.fold_in(key_list[4], 1), 0, M_DEV - 1).astype(jnp.int32),
        "edge_count": draw_edge_count(jax.random.fold_in(key_list[13], 71), part),
        "edge_weight": jnp.clip(jnp.exp(math.log(1.0) - 2.3025851 * jax.random.uniform(key_list[6], (N_GRID, N_GRID, EDGE_SLOTS), jnp.float32) ** block_levels(key_list[6], (N_GRID, N_GRID, EDGE_SLOTS), ((1, 4),), -0.2, 0.2)), 0.1, 1.0),
        "embed_weight": noise(key_list[7], (CHANNELS, D), CHANNELS ** -0.5, 0.5, ((1, 2),)),
        "attn_qkv": noise(key_list[8], (LAYERS, D, 3, D), D ** -0.5, 0.1875, ((1, 2), (3, 2))),
        "attn_out": noise(key_list[9], (LAYERS, D, D), D ** -0.5, 0.1875, ((1, 2), (2, 2))),
        "mlp_in": noise(key_list[10], (LAYERS, D, FF), D ** -0.5, 0.1875, ((1, 2), (2, 2))),
        "mlp_out": noise(key_list[11], (LAYERS, FF, D), FF ** -0.5, 0.09375, ((1, 2), (2, 2))),
        "decode_weight": noise(key_list[12], (D, CHANNELS), D ** -0.5, 0.1875, ((0, 2),)),
    }


def rms_norm(values):
    return values * lax.rsqrt(lax.optimization_barrier(jnp.mean(values * values, axis=-1, keepdims=True)) + 1e-06)

def split_sum(left, right, groups):
    group_span = left.shape[1] // groups
    summed = jnp.zeros((left.shape[0], right.shape[1]), jnp.float32)
    for group_idx in range(groups):
        lower = group_idx * group_span
        partial_value = jnp.dot(left[:, lower:lower + group_span], right[lower:lower + group_span], preferred_element_type=jnp.float32)
        summed = summed + lax.optimization_barrier(partial_value.astype(jnp.bfloat16)).astype(jnp.float32)
    return summed

def encode(grid_rows, edge_src, edge_dst, weights, embed_weight):
    offsets = jnp.arange(N_GRID, dtype=jnp.int32) * M_DEV

    def add_shard(summed, shard):
        rows_here = lax.dynamic_slice_in_dim(grid_rows, shard * GP_DEV, GP_DEV, 0)
        embedded = jax.nn.gelu(jnp.dot(rows_here, embed_weight, preferred_element_type=jnp.float32))
        picked = embedded[edge_src[shard].reshape(-1)] * weights[shard].reshape(-1)[:, None]
        targets = (edge_dst[shard] + offsets[:, None]).reshape(-1)
        return (summed + jax.ops.segment_sum(picked, targets, num_segments=MESH_NODES), None)
    summed, unused = lax.scan(add_shard, jnp.zeros((MESH_NODES, D), jnp.float32), jnp.arange(N_GRID, dtype=jnp.int32))
    return summed

def attend(queries, keys_all, values_all):
    margin = ((WINDOW, WINDOW), (0, 0), (0, 0))
    key_pad = jnp.pad(keys_all, margin)
    value_pad = jnp.pad(values_all, margin)

    def one_block(block):
        start = block * M_DEV
        q_block = lax.dynamic_slice_in_dim(queries, start, M_DEV, 0).astype(jnp.float32)
        k_block = lax.dynamic_slice_in_dim(key_pad, start, M_DEV + 2 * WINDOW, 0).astype(jnp.float32)
        v_block = lax.dynamic_slice_in_dim(value_pad, start, M_DEV + 2 * WINDOW, 0).astype(jnp.float32)
        query_pos = start + jnp.arange(M_DEV, dtype=jnp.int32)
        key_pos = start - WINDOW + jnp.arange(M_DEV + 2 * WINDOW, dtype=jnp.int32)
        visible = (jnp.abs(query_pos[:, None] - key_pos[None, :]) <= WINDOW) & (key_pos[None, :] >= 0) & (key_pos[None, :] < MESH_NODES)
        scores = jnp.einsum('qhd,khd->hqk', q_block, k_block) * HEAD_DIM ** (-0.5)
        exp_scores = jnp.where(visible[None], jnp.exp(scores), 0.0)
        shares = (exp_scores / lax.optimization_barrier(jnp.sum(exp_scores, axis=-1, keepdims=True))).astype(jnp.bfloat16)
        attended = jnp.einsum('hqk,khd->qhd', shares.astype(jnp.float32), v_block)
        return attended.astype(jnp.bfloat16).reshape(M_DEV, D)
    return lax.map(one_block, jnp.arange(N_GRID, dtype=jnp.int32)).reshape(MESH_NODES, D)

def reference(grid_state, forcing, boundary_mask, edge_src, edge_dst, edge_count, edge_weight, embed_weight, attn_qkv, attn_out, mlp_in, mlp_out, decode_weight):
    slot_ids = jnp.arange(EDGE_SLOTS, dtype=jnp.int32)
    live_slot = slot_ids[None, None, :] < edge_count[:, :, None]
    weights = jnp.where(live_slot, edge_weight, jnp.zeros_like(edge_weight))
    src_all = (edge_src + (jnp.arange(N_GRID, dtype=jnp.int32) * GP_DEV)[:, None, None]).reshape(-1)
    dst_all = (edge_dst + (jnp.arange(N_GRID, dtype=jnp.int32) * M_DEV)[None, :, None]).reshape(-1)
    weight_all = weights.reshape(-1)
    results = []
    for member in range(MEMBERS):
        grid_rows = grid_state[member]
        mesh_in = encode(grid_rows, edge_src, edge_dst, weights, embed_weight).astype(jnp.bfloat16)
        stream = mesh_in.astype(jnp.float32)
        for layer_idx in range(LAYERS):
            normed = rms_norm(stream).astype(jnp.bfloat16)
            mixed_qkv = jnp.dot(normed, attn_qkv[layer_idx].reshape(D, 3 * D), preferred_element_type=jnp.float32)
            mixed_qkv = mixed_qkv.reshape(MESH_NODES, 3, HEADS, HEAD_DIM)
            queries = rms_norm(mixed_qkv[:, 0]).astype(jnp.bfloat16)
            keys_all = rms_norm(mixed_qkv[:, 1]).astype(jnp.bfloat16)
            values_all = mixed_qkv[:, 2].astype(jnp.bfloat16)
            attended = attend(queries, keys_all, values_all)
            stream = stream + split_sum(attended, attn_out[layer_idx], N_BAND)
            normed = rms_norm(stream).astype(jnp.bfloat16)
            hidden = jax.nn.gelu(jnp.dot(normed, mlp_in[layer_idx], preferred_element_type=jnp.float32)).astype(jnp.bfloat16)
            stream = stream + split_sum(hidden, mlp_out[layer_idx], N_BAND)
        mesh_out = stream.astype(jnp.bfloat16)
        projected = jnp.dot(mesh_out, decode_weight, preferred_element_type=jnp.float32)
        decoded = jax.ops.segment_sum(projected[dst_all] * weight_all[:, None], src_all, num_segments=GRID_POINTS)
        forced = boundary_mask[:, None] == 1
        result = jnp.where(forced, forcing.astype(jnp.float32), grid_rows.astype(jnp.float32) + decoded)
        results.append(result.astype(jnp.bfloat16))
    return jnp.stack(results)
```

```python
import jax
import jax.numpy as jnp
from jax import lax
from jax.sharding import PartitionSpec as P

HEADS = 16
M_DEV = 128
WINDOW = 64
DIRECT_PEERS = 8
BF16 = jnp.bfloat16
F32 = jnp.float32


def matmul(left, right):
    return jnp.dot(left, right, preferred_element_type=F32)


def shifted(block, axes, offsets):
    sizes = [lax.axis_size(axis) for axis in axes]
    pairs = []
    total = 1
    for size in sizes:
        total *= size
    for source in range(total):
        rest, coords = source, []
        for size in reversed(sizes):
            coords.append(rest % size)
            rest //= size
        coords.reverse()
        target = 0
        for coord, offset, size in zip(coords, offsets, sizes):
            target = target * size + (coord + offset) % size
        pairs.append((source, target))
    return lax.ppermute(block, tuple(axes), pairs)


def ring(block, axis):
    count = lax.axis_size(axis)
    return [block] + [shifted(block, (axis,), (step,)) for step in range(1, count)]


def choose(options, index):
    picked = options[0]
    for at in range(1, len(options)):
        picked = jnp.where(index == at, options[at], picked)
    return picked


def rms_norm(values):
    return values * lax.rsqrt(jnp.mean(values * values, axis=-1, keepdims=True) + 1e-06)


def hi_lo(values):
    high = values.astype(BF16)
    return high, (values - high.astype(F32)).astype(BF16)


def body(
    grid_state,
    forcing,
    boundary_mask,
    edge_src,
    edge_dst,
    edge_count,
    edge_weight,
    embed_weight,
    attn_qkv,
    attn_out,
    mlp_in,
    mlp_out,
    decode_weight,
):
    shards, bands, mems = (lax.axis_size(axis) for axis in ("grid", "band", "mem"))
    grid_at, band_at, mem_at = (lax.axis_index(axis) for axis in ("grid", "band", "mem"))
    direct = shards * bands <= DIRECT_PEERS
    rows = grid_state[0]
    points, channels = rows.shape
    slots = edge_dst.shape[2]
    model_half = attn_qkv.shape[1]
    col_width = attn_qkv.shape[3]
    head_dim = model_half * mems // HEADS
    heads = col_width // head_dim
    pieces = bands // mems

    def mem_order(block, dim):
        got = ring(block, "band")
        parts = []
        for step in range(mems):
            for inner in range(pieces):
                shard = ((mem_at - step) % mems) * pieces + inner
                parts.append(choose(got, (band_at - shard) % bands))
        return jnp.concatenate(parts, axis=dim)

    def by_arrival(values):
        if not direct:
            return values
        back = values[::-1]
        return lax.dynamic_slice_in_dim(
            jnp.concatenate([back, back]), shards - 1 - grid_at, shards, 0
        )

    targets = edge_dst[:, 0]
    live = jnp.arange(slots, dtype=jnp.int32)[None, :] < edge_count[:, 0][:, None]
    weights = jnp.where(live, edge_weight[:, 0], 0.0)
    sources = jnp.pad(edge_src[0], ((1, 1), (0, 0)))
    if direct:
        towards = [(grid_at + step) % shards for step in range(shards)]
    else:
        towards = list(range(shards))
    wanted = jnp.concatenate(
        [lax.dynamic_slice_in_dim(sources, at, 3, 0).reshape(-1) for at in towards]
    )
    spread = (wanted[:, None] == jnp.arange(points, dtype=jnp.int32)[None, :]).astype(BF16)
    picked = matmul(spread, rows).astype(BF16).reshape(shards, 3 * slots, channels)
    weight_high, weight_low = hi_lo(weights)
    info = jnp.stack([targets.astype(BF16), weight_high, weight_low]).reshape(-1)
    info_rows = -(-info.size // (16 * channels)) * 16
    info = jnp.pad(info, (0, info_rows * channels - info.size)).reshape(info_rows, channels)
    if direct:
        arrived = [picked[0]]
        notes = {}
        for step in range(1, shards):
            if step in (1, shards - 1):
                message = shifted(jnp.concatenate([picked[step], info]), ("grid",), (step,))
                notes[step] = message[3 * slots :]
                arrived.append(message[: 3 * slots])
            else:
                arrived.append(shifted(picked[step], ("grid",), (step,)))
        arrived = jnp.concatenate(arrived)
        below, above = notes[1], notes[shards - 1]
    else:
        message = jnp.concatenate(
            [picked, jnp.broadcast_to(info[None], (shards,) + info.shape)], axis=1
        )
        message = lax.all_to_all(message, "grid", 0, 0, tiled=True)
        arrived = message[:, : 3 * slots].reshape(-1, channels)
        below = message[(grid_at - 1) % shards, 3 * slots :]
        above = message[(grid_at + 1) % shards, 3 * slots :]

    def unpack(note, inside):
        note = note.reshape(-1)[: 3 * shards * slots].reshape(3, shards, slots).astype(F32)
        return note[0].astype(jnp.int32), jnp.where(inside, note[1] + note[2], 0.0)

    embed_full = mem_order(embed_weight, 1)
    qkv_parts = ring(attn_qkv[0], "mem")
    out_parts = ring(attn_out[0], "mem")
    in_parts = ring(mlp_in[0], "mem")
    decode_full = mem_order(decode_weight, 0)
    folded = ring(matmul(mlp_out[0], decode_full[:model_half]), "mem")
    folded = sum(folded[1:], folded[0]).astype(BF16)

    below_dst, below_weight = unpack(below, grid_at > 0)
    above_dst, above_weight = unpack(above, grid_at < shards - 1)
    places = jnp.stack([below_dst - M_DEV, targets, above_dst + M_DEV], axis=1) + WINDOW
    place_weights = jnp.stack([below_weight, weights, above_weight], axis=1)
    places = by_arrival(places).reshape(-1)
    place_weights = by_arrival(place_weights).reshape(-1)
    extent = M_DEV + 2 * WINDOW
    collect = jnp.where(
        jnp.arange(extent, dtype=jnp.int32)[:, None] == places[None, :], place_weights[None, :], 0.0
    )
    collect_high, collect_low = hi_lo(collect)
    embedded = jax.nn.gelu(matmul(arrived, embed_full)).astype(BF16)
    mesh_in = (matmul(collect_high, embedded) + matmul(collect_low, embedded)).astype(BF16)
    wide_stream = mesh_in.astype(F32)

    normed = rms_norm(wide_stream).astype(BF16)
    mixed = sum(
        matmul(
            normed[:, step * model_half : (step + 1) * model_half],
            part.reshape(model_half, 3 * col_width),
        )
        for step, part in enumerate(qkv_parts)
    ).reshape(extent, 3, heads, head_dim)
    queries = rms_norm(mixed[WINDOW : WINDOW + M_DEV, 0]).astype(BF16)
    keys = rms_norm(mixed[:, 1]).astype(BF16)
    values = mixed[:, 2].astype(BF16)
    query_pos = grid_at * M_DEV + jnp.arange(M_DEV, dtype=jnp.int32)
    key_pos = grid_at * M_DEV - WINDOW + jnp.arange(extent, dtype=jnp.int32)
    visible = (
        (jnp.abs(query_pos[:, None] - key_pos[None, :]) <= WINDOW)
        & (key_pos[None, :] >= 0)
        & (key_pos[None, :] < M_DEV * shards)
    )
    scores = jnp.einsum("qhd,khd->hqk", queries, keys, preferred_element_type=F32) * head_dim ** (
        -0.5
    )
    exp_scores = jnp.where(visible[None], jnp.exp(scores), 0.0)
    shares = (exp_scores / jnp.sum(exp_scores, axis=-1, keepdims=True)).astype(BF16)
    attended = jnp.einsum("hqk,khd->qhd", shares, values, preferred_element_type=F32)
    attended = attended.astype(BF16).reshape(M_DEV, col_width)
    product = jnp.concatenate([matmul(attended, part) for part in out_parts], axis=1).astype(BF16)
    products = ring(product, "band")
    stream = wide_stream[WINDOW : WINDOW + M_DEV]
    stream = stream + sum(part.astype(F32) for part in products)

    normed = rms_norm(stream).astype(BF16)
    hidden = jax.nn.gelu(
        sum(
            matmul(normed[:, step * model_half : (step + 1) * model_half], part)
            for step, part in enumerate(in_parts)
        )
    ).astype(BF16)
    carried = jnp.where(band_at == 0, stream, 0.0).astype(BF16)
    projected = (matmul(hidden, folded) + matmul(carried, decode_full)).astype(BF16)
    reach = (
        targets.reshape(-1)[:, None] == jnp.arange(M_DEV, dtype=jnp.int32)[None, :]
    ).astype(BF16)
    outgoing = (matmul(reach, projected) * weights.reshape(-1)[:, None]).astype(BF16)
    outgoing = outgoing.reshape(shards, slots, channels)
    if direct:
        returned = []
        for band_step in range(bands):
            for step in range(shards):
                block = lax.dynamic_index_in_dim(
                    outgoing, (grid_at + step) % shards, 0, keepdims=False
                )
                if step or band_step:
                    block = shifted(block, ("grid", "band"), (step, band_step))
                returned.append(block)
        returned = jnp.concatenate(returned)
        copies = bands
    else:
        summed = sum(part.astype(F32) for part in ring(outgoing, "band"))
        returned = lax.all_to_all(summed.astype(BF16), "grid", 0, 0, tiled=True)
        returned = returned.reshape(-1, channels)
        copies = 1
    home = by_arrival(edge_src[0]).reshape(-1)
    scatter = (jnp.arange(points, dtype=jnp.int32)[:, None] == home[None, :]).astype(BF16)
    decoded = matmul(jnp.concatenate([scatter] * copies, axis=1), returned)
    forced = boundary_mask[:, None] == 1
    result = jnp.where(forced, forcing.astype(F32), rows.astype(F32) + decoded)
    return result.astype(BF16)[None]


def solution(mesh):
    return jax.shard_map(
        body,
        mesh=mesh,
        in_specs=(
            P(("dom", "mem"), "grid", None),
            P(("dom", "grid"), None),
            P("grid"),
            P("grid", None, None),
            P(None, "grid", None),
            P(None, "grid"),
            P(None, "grid", None),
            P(None, "band"),
            P(None, "mem", None, "band"),
            P(None, "band", "mem"),
            P(None, "mem", "band"),
            P(None, "band", "mem"),
            P("band", None),
        ),
        out_specs=P(("dom", "mem"), "grid", None),
        check_vma=False,
    )
```

```python
import functools

import jax
import jax.numpy as jnp
from jax import lax
from jax.experimental import pallas as pl
from jax.experimental.pallas import tpu as pltpu
from jax.sharding import PartitionSpec as P

HEADS = 16
M_DEV = 128
WINDOW = 64
EXTENT = M_DEV + 2 * WINDOW
DIRECT_PEERS = 8
CHUNKS = 4
LANES = 128
BF16 = jnp.bfloat16
F32 = jnp.float32
VMEM = pl.BlockSpec(memory_space=pltpu.VMEM)
ANY = pl.BlockSpec(memory_space=pl.ANY)


def matmul(left, right):
    return jnp.dot(left, right, preferred_element_type=F32)


def matmul_rows(left, right):
    return lax.dot_general(left, right, (((0,), (0,)), ((), ())), preferred_element_type=F32)


def matmul_cols(left, right):
    return lax.dot_general(left, right, (((1,), (1,)), ((), ())), preferred_element_type=F32)


def shifted(block, axis, step):
    count = lax.axis_size(axis)
    return lax.ppermute(block, axis, [(at, (at + step) % count) for at in range(count)])


def ring(block, axis):
    return [block] + [shifted(block, axis, step) for step in range(1, lax.axis_size(axis))]


def choose(options, index):
    picked = options[0]
    for at in range(1, len(options)):
        picked = jnp.where(index == at, options[at], picked)
    return picked


def mem_order(got, mems):
    bands = len(got)
    band_at, mem_at = lax.axis_index("band"), lax.axis_index("mem")
    pieces = bands // mems
    parts = []
    for step in range(mems):
        for inner in range(pieces):
            shard = lax.rem(mem_at - step + mems, mems) * pieces + inner
            parts.append(choose(got, lax.rem(band_at - shard + bands, bands)))
    return parts


def rms_norm(values):
    return values * lax.rsqrt(jnp.mean(values * values, axis=-1, keepdims=True) + 1e-06)


def hi_lo(values):
    high = values.astype(BF16)
    return high, (values - high.astype(F32)).astype(BF16)


def iota(shape, dim):
    return lax.broadcasted_iota(jnp.int32, shape, dim)


def column(values):
    count, slots = values.shape
    tall = jnp.concatenate(
        [jnp.broadcast_to(values[at : at + 1], (slots, slots)) for at in range(count)]
    )
    own = lax.rem(iota(tall.shape, 0), slots) == iota(tall.shape, 1)
    return jnp.sum(jnp.where(own, tall, 0.0), axis=1, keepdims=True)


def live_weights(count_ref, weight_ref):
    weights = weight_ref[...]
    return jnp.where(iota(weights.shape, 1) < count_ref[...], weights, 0.0)


def pick_kernel(src_ref, rows_ref, dst_ref, count_ref, weight_ref, *rest):
    outs, padded, note = rest[:-2], rest[-2], rest[-1]
    shards, slots = src_ref.shape
    span = shards * slots
    grid_at = lax.axis_index("grid")
    home = column(src_ref[...].astype(F32))
    spread = (home == iota((span, rows_ref.shape[0]), 1).astype(F32)).astype(BF16)
    edge = jnp.zeros((slots, rows_ref.shape[1]), BF16)
    padded[0:slots] = edge
    padded[slots : slots + span] = matmul(spread, rows_ref[...]).astype(BF16)
    padded[slots + span :] = edge
    weights = live_weights(count_ref, weight_ref)
    high = weights.astype(BF16).astype(F32)
    note[...] = jnp.zeros(note.shape, F32)
    note[0:shards, 0:slots] = dst_ref[...].astype(F32)
    note[shards : 2 * shards, 0:slots] = high
    note[2 * shards : 3 * shards, 0:slots] = weights - high
    packed = note[...].astype(BF16)
    for at, out in enumerate(outs):
        towards = lax.rem(grid_at + at, shards) if len(outs) <= DIRECT_PEERS else at
        out[0 : 3 * slots] = padded[pl.ds(pl.multiple_of(towards * slots, slots), 3 * slots)]
        out[3 * slots :] = packed


def attend_kernel(shards, bands, mems, direct, *refs):
    refs = list(refs)
    messages = [refs.pop(0) for _ in range(shards)]
    below, above, dst_ref, count_ref, weight_ref = (refs.pop(0) for _ in range(5))
    embeds = [refs.pop(0) for _ in range(bands)]
    qkv_hbm = [refs.pop(0) for _ in range(mems)]
    out_hbm = [refs.pop(0) for _ in range(mems)]
    product_ref, resid_ref, arrived, qkv, proj, sems = refs
    slots = dst_ref.shape[1]
    grid_at = lax.axis_index("grid")
    copies = [pltpu.make_async_copy(s, qkv.at[i], sems.at[i]) for i, s in enumerate(qkv_hbm)]
    copies += [
        pltpu.make_async_copy(s, proj.at[i], sems.at[mems + i]) for i, s in enumerate(out_hbm)
    ]
    for copy in copies:
        copy.start()

    for step, message in enumerate(messages):
        origin = lax.rem(grid_at - step + shards, shards) if direct else step
        arrived[pl.ds(pl.multiple_of(origin * 3 * slots, 3 * slots), 3 * slots)] = message[
            0 : 3 * slots
        ]
    places, loads = [], []
    for offset, message in ((-M_DEV, below), (0, None), (M_DEV, above)):
        if message is None:
            places.append(dst_ref[...].astype(F32) + WINDOW)
            loads.append(live_weights(count_ref, weight_ref))
        else:
            inside = grid_at > 0 if offset < 0 else grid_at < shards - 1
            note = message[3 * slots :].astype(F32)
            places.append(note[0:shards, 0:slots] + (WINDOW + offset))
            load = note[shards : 2 * shards, 0:slots] + note[2 * shards : 3 * shards, 0:slots]
            loads.append(jnp.where(inside, load, 0.0))
    order = [(c, s) for s in range(shards) for c in range(3)]
    place = column(jnp.concatenate([places[c][s : s + 1] for c, s in order]))
    load = column(jnp.concatenate([loads[c][s : s + 1] for c, s in order]))
    spread = jnp.where(place == iota((place.shape[0], EXTENT), 1).astype(F32), load, 0.0)
    spread_high, spread_low = hi_lo(spread)
    embed = jnp.concatenate(mem_order([ref[...] for ref in embeds], mems), axis=1)
    embedded = jax.nn.gelu(matmul(arrived[...], embed)).astype(BF16)
    mesh_in = matmul_rows(spread_high, embedded) + matmul_rows(spread_low, embedded)
    mesh_in = mesh_in.astype(BF16)
    resid_ref[...] = mesh_in[WINDOW : WINDOW + M_DEV]
    normed = rms_norm(mesh_in.astype(F32)).astype(BF16)

    half = qkv.shape[2]
    width = qkv.shape[3]
    head_dim = half * mems // HEADS
    for copy in copies[:mems]:
        copy.wait()

    def project(rows, which):
        return sum(
            matmul(rows[:, step * half : (step + 1) * half], qkv[step, which])
            for step in range(mems)
        )

    queries = project(normed[WINDOW : WINDOW + M_DEV], 0)
    keys = project(normed, 1)
    values = project(normed, 2).astype(BF16)
    group = LANES // head_dim
    same = (iota((LANES, LANES), 0) // head_dim == iota((LANES, LANES), 1) // head_dim).astype(BF16)
    lane_head = iota((M_DEV, LANES), 1) // head_dim

    def head_norm(block):
        mean = matmul((block * block).astype(BF16), same) * (1.0 / head_dim)
        return (block * lax.rsqrt(mean + 1e-06)).astype(BF16)

    row = iota((M_DEV, EXTENT), 0)
    col = iota((M_DEV, EXTENT), 1)
    key_pos = grid_at * M_DEV - WINDOW + col
    visible = (
        (jnp.abs(row + WINDOW - col) <= WINDOW) & (key_pos >= 0) & (key_pos < M_DEV * shards)
    )
    visible = jnp.concatenate([visible.astype(F32)] * group)
    attended = []
    for block in range(width // LANES):
        lanes = slice(block * LANES, (block + 1) * LANES)
        query = head_norm(queries[:, lanes])
        key = head_norm(keys[:, lanes])
        stacked = jnp.concatenate(
            [jnp.where(lane_head == head, query, jnp.zeros_like(query)) for head in range(group)]
        )
        scores = matmul_cols(stacked, key) * head_dim ** (-0.5)
        weights = jnp.exp(scores) * visible
        shares = (weights / jnp.sum(weights, axis=-1, keepdims=True)).astype(BF16)
        mixed = matmul(shares, values[:, lanes])
        attended.append(
            choose([mixed[head * M_DEV : (head + 1) * M_DEV] for head in range(group)], lane_head)
        )
    attended = jnp.concatenate(attended, axis=1).astype(BF16)
    for copy in copies[mems:]:
        copy.wait()
    for step in range(mems):
        product_ref[:, step * half : (step + 1) * half] = matmul(attended, proj[step]).astype(BF16)


def fold_kernel(back_ref, *refs):
    decodes, out_ref = refs[:-1], refs[-1]
    mems = lax.axis_size("mem")
    decode = jnp.concatenate(mem_order([ref[...] for ref in decodes], mems)[: len(decodes) // mems])
    out_ref[...] = matmul(back_ref[...], decode)


def finish_kernel(shards, bands, mems, copies_out, *refs):
    refs = list(refs)
    products = [refs.pop(0) for _ in range(bands)]
    resid_ref = refs.pop(0)
    in_hbm = [refs.pop(0) for _ in range(mems)]
    folds = [refs.pop(0) for _ in range(mems)]
    decodes = [refs.pop(0) for _ in range(bands)]
    dst_ref, count_ref, weight_ref, out_ref, weight_in, sems = refs
    half, hidden_width = weight_in.shape[1:]
    step_width = hidden_width // CHUNKS
    slots = dst_ref.shape[1]

    def fetch(chunk, at):
        lanes = pl.ds(chunk * step_width, step_width)
        return pltpu.make_async_copy(
            in_hbm[at].at[:, lanes], weight_in.at[at, :, lanes], sems.at[chunk, at]
        )

    for chunk in range(CHUNKS):
        for at in range(mems):
            fetch(chunk, at).start()
    stream = resid_ref[...].astype(F32) + sum(ref[...].astype(F32) for ref in products)
    normed = rms_norm(stream).astype(BF16)
    reach = (column(dst_ref[...].astype(F32)) == iota((shards * slots, M_DEV), 1).astype(F32)).astype(
        BF16
    )
    load = column(live_weights(count_ref, weight_ref))
    carried = jnp.where(lax.axis_index("band") == 0, stream, 0.0).astype(BF16)
    decode = jnp.concatenate(mem_order([ref[...] for ref in decodes], mems))
    projected = matmul(carried, decode)
    for chunk in range(CHUNKS):
        lanes = slice(chunk * step_width, (chunk + 1) * step_width)
        for at in range(mems):
            fetch(chunk, at).wait()
        hidden = jax.nn.gelu(
            sum(
                matmul(normed[:, at * half : (at + 1) * half], weight_in[at, :, lanes])
                for at in range(mems)
            )
        ).astype(BF16)
        fold = sum(ref[lanes, :] for ref in folds).astype(BF16)
        projected = projected + matmul(hidden, fold)
    outgoing = (matmul(reach, projected.astype(BF16)) * load).astype(BF16)
    for shard in range(shards):
        for at in range(copies_out):
            out_ref[shard * copies_out + at] = outgoing[shard * slots : (shard + 1) * slots]


def body(
    grid_state,
    forcing,
    boundary_mask,
    edge_src,
    edge_dst,
    edge_count,
    edge_weight,
    embed_weight,
    attn_qkv,
    attn_out,
    mlp_in,
    mlp_out,
    decode_weight,
):
    shards, bands, mems = (lax.axis_size(axis) for axis in ("grid", "band", "mem"))
    direct = shards <= DIRECT_PEERS
    grid_at = lax.axis_index("grid")
    rows = grid_state[0]
    points, channels = rows.shape
    sources, targets, weights = edge_src[0], edge_dst[:, 0], edge_weight[:, 0]
    slots = targets.shape[1]
    qkv_own = jnp.transpose(attn_qkv[0], (1, 0, 2))
    half, width = qkv_own.shape[1:]
    model = half * mems
    edges = (targets, edge_count, weights)
    note_rows = -(-3 * shards // 16) * 16
    message_shape = jax.ShapeDtypeStruct((3 * slots + note_rows, channels), BF16)

    messages = pl.pallas_call(
        pick_kernel,
        out_shape=[message_shape] * shards,
        in_specs=[VMEM] * 5,
        out_specs=[VMEM] * shards,
        scratch_shapes=[
            pltpu.VMEM(((shards + 2) * slots, channels), BF16),
            pltpu.VMEM((note_rows, channels), F32),
        ],
        name="pick",
    )(sources, rows, *edges)
    if direct:
        messages = [messages[0]] + [
            shifted(messages[step], "grid", step) for step in range(1, shards)
        ]
        below, above = messages[1 % shards], messages[shards - 1]
    else:
        stacked = lax.all_to_all(jnp.stack(messages), "grid", 0, 0, tiled=True)
        messages = [stacked[at] for at in range(shards)]
        below = stacked[(grid_at - 1) % shards]
        above = stacked[(grid_at + 1) % shards]

    embeds = ring(embed_weight, "band")
    qkv_parts = ring(qkv_own, "mem")
    out_parts = ring(attn_out[0], "mem")
    in_parts = ring(mlp_in[0], "mem")
    decodes = ring(decode_weight, "band")
    back = mlp_out[0]
    folded = pl.pallas_call(
        fold_kernel,
        out_shape=jax.ShapeDtypeStruct((back.shape[0], channels), F32),
        in_specs=[VMEM] * (1 + bands),
        out_specs=VMEM,
        name="fold",
    )(back, *decodes)
    folds = ring(folded, "mem")

    product, resid = pl.pallas_call(
        functools.partial(attend_kernel, shards, bands, mems, direct),
        out_shape=[jax.ShapeDtypeStruct((M_DEV, model), BF16)] * 2,
        in_specs=[VMEM] * (shards + 5 + bands) + [ANY] * (2 * mems),
        out_specs=[VMEM] * 2,
        scratch_shapes=[
            pltpu.VMEM((shards * 3 * slots, channels), BF16),
            pltpu.VMEM((mems, 3, half, width), BF16),
            pltpu.VMEM((mems, width, half), BF16),
            pltpu.SemaphoreType.DMA((2 * mems,)),
        ],
        name="attend",
    )(*messages, below, above, *edges, *embeds, *qkv_parts, *out_parts)
    products = ring(product, "band")

    hidden_width = mlp_in.shape[2]
    copies_out = bands if direct else 1
    outgoing = pl.pallas_call(
        functools.partial(finish_kernel, shards, bands, mems, copies_out),
        out_shape=jax.ShapeDtypeStruct((shards * copies_out, slots, channels), BF16),
        in_specs=[VMEM] * (bands + 1) + [ANY] * mems + [VMEM] * (mems + bands + 3),
        out_specs=VMEM,
        scratch_shapes=[
            pltpu.VMEM((mems, half, hidden_width), BF16),
            pltpu.SemaphoreType.DMA((CHUNKS, mems)),
        ],
        name="finish",
    )(*products, resid, *in_parts, *folds, *decodes, *edges)
    if direct:
        returned = lax.all_to_all(outgoing, ("grid", "band"), 0, 0, tiled=True)
    else:
        summed = sum(part.astype(F32) for part in ring(outgoing, "band"))
        returned = lax.all_to_all(summed.astype(BF16), "grid", 0, 0, tiled=True)
    returned = returned.reshape(-1, channels)

    home = jnp.broadcast_to(sources[:, None, :], (shards, copies_out, slots)).reshape(-1)
    forced = boundary_mask[:, None] == 1
    place = jnp.arange(points, dtype=jnp.int32)[:, None]
    scatter = ((place == home[None, :]) & ~forced).astype(BF16)
    base = jnp.where(forced, forcing, rows)
    return (base.astype(F32) + matmul(scatter, returned)).astype(BF16)[None]


def solution(mesh):
    return jax.shard_map(
        body,
        mesh=mesh,
        in_specs=(
            P(("dom", "mem"), "grid", None),
            P(("dom", "grid"), None),
            P("grid"),
            P("grid", None, None),
            P(None, "grid", None),
            P(None, "grid"),
            P(None, "grid", None),
            P(None, "band"),
            P(None, "mem", None, "band"),
            P(None, "band", "mem"),
            P(None, "mem", "band"),
            P(None, "band", "mem"),
            P("band", None),
        ),
        out_specs=P(("dom", "mem"), "grid", None),
        check_vma=False,
    )
```
